32 devices in a mesh: group: 2 (over y), ctx: 4 (over z), head: 2 (over x), rep: 2 (over core).
Axes of the slice: x: 2, y: 2, z: 4, core: 2. Of those that a mesh axis runs over, the one named last changes fastest.
Arguments:
- signal_input: bfloat16 [3072, 4096], P(('group', 'ctx'), ('head', 'rep')), parts along dimension 0, may hold values from -6 to 6
- gate_input: bfloat16 [3072, 4096], P(('group', 'ctx'), ('head', 'rep')), parts along dimension 0, may hold values from -6 to 6
- coupling_input: bfloat16 [3072, 2, 256], P(('group', 'ctx'), None, 'head'), parts along dimension 0, may hold values from -6 to 6
- step_input: float32 [64, 3072], P(('head', 'rep'), ('group', 'ctx')), parts along dimension 1, may hold values from -5 to 5
- signal_taps: float32 [4, 4096], P(None, ('head', 'rep')), may hold values from -3 to 3
- coupling_taps: float32 [4, 2, 256], P(None, None, 'head'), may hold values from -3 to 3
- step_bias: float32 [64], P(('head', 'rep')), may hold values from -1 to 1
- head_decay_rate: float32 [64], P(('head', 'rep')), may hold values from 1.30208333e-05 to 0.04
- head_skip_gain: float32 [64], P(('head', 'rep')), may hold values from 0.5 to 1.5
- gated_norm_gain: float32 [4096], P(('head', 'rep')), may hold values from 0.25 to 1.75
- request_adapter: int32 [2], P('group'), parts along dimension 0, may hold values from 0 to 7
- stored_down_weight: bfloat16 [8, 64, 4096], P('rep', None, 'head'), may hold values from -0.09375 to 0.09375
- stored_up_weight: bfloat16 [8, 64, 8192], P('rep', None, 'head'), may hold values from -0.75 to 0.75
Outputs:
- mixer_out: bfloat16 [3072, 4096], P(('group', 'ctx'), ('head', 'rep')), parts along dimension 0
- adapter_delta: bfloat16 [3072, 8192], P(('group', 'ctx'), ('head', 'rep')), parts along dimension 0
The draws below stay inside these ranges and needn't reach their ends.
There are 2 independent parts, one for each index of `group`. The reference program is written for one: setup_inputs(seed, part) draws one part's arguments, and reference() takes and returns one part's arrays. A program takes and returns all parts, laid end to end along the dimension named above; an argument that names none is the same for every part. Nothing has to cross between parts.
All inputs are finite; a program needn't handle non-finite values.
Results may differ from the reference program's by a relative error of at most 0.015.
Values may be sent and summed in bfloat16 or wider, within the bound.
A program may use at most 64 MiB of HBM per device.

```python
import jax
import jax.numpy as jnp
from jax import lax

MODEL_WIDTH = 8192
P_SIZE = 64
N = 128
KW = 4
ADAPTER_RANK = 64
HPG = 32
BLOCK = 128
SEQS = 1
ADAPTER_COUNT = 8
HEADS = 64
GROUPS = 2
INNER_CHANNELS = 4096
LENGTH = 1536
TOKENS = 1536


def draw_head_decay_rate(key, part):
    lowest = 0.02 / LENGTH
    highest = 0.04
    mixing = jax.random.uniform(key, (HEADS,), jnp.float32)
    return jnp.exp(jnp.log(lowest) + mixing * (jnp.log(highest) - jnp.log(lowest))).astype(jnp.float32)


def block_scale(key, extent, cuts, least, top_value):
    factor_of, own = 1.0, jax.random.fold_in(key, 6)
    for dim, shards_of in cuts:
        steps = jnp.exp(jax.random.uniform(jax.random.fold_in(own, dim), (shards_of,), jnp.float32, least / len(cuts), top_value / len(cuts)))
        factor_of = factor_of * jnp.repeat(steps, extent[dim] // shards_of).reshape([-1 if axis == dim else 1 for axis in range(len(extent))])
    return factor_of


def normal_values(own_key, extent, scale, most, cuts=(), kind=jnp.bfloat16):
    result = jax.random.normal(own_key, extent, jnp.float32) * scale
    if len(cuts) > 0:
        result = block_scale(own_key, extent, cuts, -0.22, 0.18) * result
    return jnp.clip(result, min=-most, max=most).astype(kind)


def setup_inputs(seed: int = 0, part: int = 0) -> dict:
    key_list = jax.random.split(jax.random.key(seed), 14)
    part_splits = jax.random.split(jax.random.fold_in(key_list[13], part), 14)
    return {
        "signal_input": normal_values(part_splits[0], (TOKENS, INNER_CHANNELS), 1.0, 6.0, ((0, 4), (1, 4))),
        "gate_input": normal_values(part_splits[1], (TOKENS, INNER_CHANNELS), 1.0, 6.0, ((0, 4), (1, 4))),
        "coupling_input": normal_values(part_splits[2], (TOKENS, 2, GROUPS * N), 1.0, 6.0, ((0, 4), (2, 2))),
        "step_input": normal_values(part_splits[3], (HEADS, TOKENS), 1.0, 5.0, ((0, 4), (1, 4)), jnp.float32),
        "signal_taps": normal_values(key_list[4], (KW, INNER_CHANNELS), KW ** -0.5, 3.0, ((1, 4),), jnp.float32),
        "coupling_taps": normal_values(key_list[5], (KW, 2, GROUPS * N), KW ** -0.5, 3.0, ((2, 2),), jnp.float32),
        "step_bias": jnp.clip(jax.random.uniform(key_list[6], (HEADS,), jnp.float32, -1.0, 1.0) * block_scale(key_list[6], (HEADS,), ((0, 4),), -0.4, 0.0), -1.0, 1.0),
        "head_decay_rate": draw_head_decay_rate(jax.random.fold_in(key_list[13], 71), part),
        "head_skip_gain": jnp.clip(0.5 + 1.0 * jax.random.uniform(key_list[8], (HEADS,), jnp.float32) ** block_scale(key_list[8], (HEADS,), ((0, 4),), -0.2, 0.2), 0.5, 1.5),
        "gated_norm_gain": jnp.clip(1.0 + 0.15 * jax.random.normal(key_list[9], (INNER_CHANNELS,), jnp.float32), 0.25, 1.75),
        "request_adapter": jax.random.randint(part_splits[10], (SEQS,), 0, ADAPTER_COUNT).astype(jnp.int32),
        "stored_down_weight": normal_values(key_list[11], (ADAPTER_COUNT, ADAPTER_RANK, INNER_CHANNELS), INNER_CHANNELS ** -0.5, 0.09375, ((0, 2), (2, 2))),
        "stored_up_weight": normal_values(key_list[12], (ADAPTER_COUNT, ADAPTER_RANK, MODEL_WIDTH), ADAPTER_RANK ** -0.5, 0.75, ((0, 2), (2, 2))),
    }


epsilon = 1e-05

def causal_conv(values, weight):
    width = values.shape[-1]
    sequence = values.reshape(SEQS, LENGTH, width).astype(jnp.float32)
    padded = jnp.pad(sequence, ((0, 0), (KW - 1, 0), (0, 0)))
    total = jnp.zeros(sequence.shape, jnp.float32)
    for offset in range(KW):
        total = total + weight[offset] * padded[:, offset:offset + LENGTH]
    return jax.nn.silu(total).reshape(TOKENS, width).astype(jnp.bfloat16)

def reference(signal_input, gate_input, coupling_input, step_input, signal_taps, coupling_taps, step_bias, head_decay_rate, head_skip_gain, gated_norm_gain, request_adapter, stored_down_weight, stored_up_weight):
    x_conv = causal_conv(signal_input, signal_taps)
    bc_conv = causal_conv(coupling_input.reshape(TOKENS, 2 * GROUPS * N), coupling_taps.reshape(KW, 2 * GROUPS * N))
    bc_conv = bc_conv.reshape(TOKENS, 2, GROUPS, N)
    blocks = TOKENS // BLOCK
    step_size = jax.nn.softplus(step_input + step_bias[:, None])
    log_decay = -step_size * head_decay_rate[:, None]
    cumulative = jnp.cumsum(log_decay.reshape(HEADS, blocks, BLOCK), axis=-1).transpose(1, 0, 2)
    steps_blocked = step_size.reshape(HEADS, blocks, BLOCK).transpose(1, 0, 2)
    x_blocks = x_conv.reshape(blocks, BLOCK, HEADS, P_SIZE)
    b_blocks = bc_conv[:, 0].reshape(blocks, BLOCK, GROUPS, N)
    c_blocks = bc_conv[:, 1].reshape(blocks, BLOCK, GROUPS, N)
    starts = (jnp.arange(blocks) % (LENGTH // BLOCK) == 0).astype(jnp.float32)
    causal = jnp.tril(jnp.ones((BLOCK, BLOCK), bool))

    def advance(state, inputs):
        x_block, b_block, c_block, cum_block, dt_block, start = inputs
        state = state * (1.0 - start)
        scores = jnp.einsum('ign,jgn->gij', c_block.astype(jnp.float32), b_block.astype(jnp.float32))
        scores = jnp.repeat(scores, HPG, axis=0)
        log_gap = cum_block[:, :, None] - cum_block[:, None, :]
        weights = jnp.where(causal, scores * jnp.exp(jnp.where(causal, log_gap, 0.0)) * dt_block[:, None, :], 0.0)
        weights = lax.optimization_barrier(weights.astype(jnp.bfloat16)).astype(jnp.float32)
        y_diag = jnp.einsum('hij,jhp->ihp', weights, x_block.astype(jnp.float32))
        b_heads = jnp.repeat(b_block, HPG, axis=1).astype(jnp.float32)
        tail_decay = jnp.exp(cum_block[:, -1:] - cum_block) * dt_block
        b_weighted = tail_decay.T[:, :, None] * b_heads
        b_weighted = lax.optimization_barrier(b_weighted.astype(jnp.bfloat16)).astype(jnp.float32)
        pieces = jnp.einsum('jhp,jhn->hpn', x_block.astype(jnp.float32), b_weighted)
        c_heads = jnp.repeat(c_block, HPG, axis=1).astype(jnp.float32)
        entering = lax.optimization_barrier(state.astype(jnp.bfloat16)).astype(jnp.float32)
        y_carried = jnp.einsum('ihn,hpn->ihp', c_heads, entering) * jnp.exp(cum_block).T[:, :, None]
        outputs = y_diag + y_carried + head_skip_gain[None, :, None] * x_block.astype(jnp.float32)
        state = jnp.exp(cum_block[:, -1])[:, None, None] * state + pieces
        return (state, outputs)
    _, outputs = lax.scan(advance, jnp.zeros((HEADS, P_SIZE, N), jnp.float32), (x_blocks, b_blocks, c_blocks, cumulative, steps_blocked, starts))
    y_full = outputs.reshape(TOKENS, INNER_CHANNELS)
    gated = y_full * jax.nn.silu(gate_input.astype(jnp.float32))
    grouped = gated.reshape(TOKENS, GROUPS, HPG * P_SIZE)
    inverse = lax.rsqrt(lax.optimization_barrier(jnp.mean(grouped * grouped, axis=-1)) + epsilon)
    mixer_out = ((grouped * inverse[:, :, None]).reshape(TOKENS, INNER_CHANNELS) * gated_norm_gain).astype(jnp.bfloat16)
    request_updates = mixer_out.reshape(SEQS, LENGTH, INNER_CHANNELS)
    adapter_updates = []
    for request_index in range(SEQS):
        stored_tables = request_adapter[request_index]
        reduced_output = jnp.dot(request_updates[request_index], stored_down_weight[stored_tables].T, preferred_element_type=jnp.float32).astype(jnp.bfloat16)
        adapter_updates.append(jnp.dot(reduced_output, stored_up_weight[stored_tables], preferred_element_type=jnp.float32).astype(jnp.bfloat16))
    return (mixer_out, jnp.concatenate(adapter_updates, axis=0))
```

```python
import functools

import jax
import jax.numpy as jnp
from jax import lax
from jax.experimental import pallas as pl
from jax.experimental.pallas import tpu as pltpu
from jax.sharding import PartitionSpec as P

BLOCK = 128
MESH = pl.DeviceIdType.MESH
HALO = 16
PARTS = 4
EDGE = 8
epsilon = 1e-05


def silu(value):
    half = 0.5 * value
    return half * jnp.tanh(half) + half


def split(value, terms):
    parts = []
    for _ in range(terms):
        top = value.astype(jnp.bfloat16)
        parts.append(top)
        value = value - top.astype(jnp.float32)
    return jnp.concatenate(parts, axis=0)


def column(row):
    size = row.shape[1]
    eye = lax.broadcasted_iota(jnp.int32, (size, size), 0) == lax.broadcasted_iota(
        jnp.int32, (size, size), 1
    )
    spread = jnp.broadcast_to(row, (size, size))
    return jnp.sum(jnp.where(eye, spread, 0.0), axis=1, keepdims=True)


def kernel(
    sizes,
    adapter_hbm,
    signal_hbm,
    gate_hbm,
    coupling_hbm,
    down_hbm,
    up_hbm,
    step_hbm,
    signal_taps_hbm,
    coupling_taps_hbm,
    step_bias_hbm,
    rate_hbm,
    skip_hbm,
    norm_gain_hbm,
    mixer_ref,
    reduced_ref,
    up_mine,
    signal,
    gate,
    coupling,
    down_table,
    up_table,
    tail_x,
    halo_out,
    halo_in,
    pad_x,
    pad_bc,
    conv_x,
    rhs,
    lhs,
    b_turned,
    grow,
    local_y,
    final,
    piece_ref,
    b_keep,
    wide_ref,
    decay_ref,
    adapter_ref,
    state_out,
    state_in,
    down_out,
    down_in,
    down_mine,
    up_out,
    up_in,
    low_all,
    square_all,
    step_ref,
    signal_taps_ref,
    coupling_taps_ref,
    step_bias_ref,
    rate_ref,
    skip_ref,
    norm_gain_ref,
    load_sem,
    halo_send,
    halo_recv,
    table_send,
    table_recv,
    state_send,
    state_recv,
    low_send,
    low_recv,
    square_send,
    square_recv,
):
    ctx_count, head_count, rep_count, chunk = sizes
    ctx, head, rep = (lax.axis_index(name) for name in ("ctx", "head", "rep"))
    rows, channels = signal.shape
    heads = step_ref.shape[0]
    head_size = channels // heads
    n = coupling.shape[2]
    taps = signal_taps_ref.shape[0]
    blocks = rows // BLOCK
    chunks = channels // chunk
    rank = down_mine.shape[0]
    up_width = up_in.shape[2]
    first, last = ctx == 0, ctx == ctx_count - 1
    f32, bf16 = jnp.float32, jnp.bfloat16

    segment = channels // 4
    copies = [
        (step_hbm, step_ref),
        (step_bias_hbm, step_bias_ref),
        (rate_hbm, rate_ref),
        (coupling_hbm, coupling),
        (coupling_taps_hbm, coupling_taps_ref),
        (signal_hbm.at[pl.ds(rows - HALO, HALO)], tail_x),
        (signal_taps_hbm, signal_taps_ref),
    ]
    signal_at = len(copies)
    for c in range(chunks):
        lanes = pl.ds(c * chunk, chunk)
        copies.append((signal_hbm.at[:, lanes], signal.at[:, lanes]))
    later = len(copies)
    copies += [
        (skip_hbm, skip_ref),
        (norm_gain_hbm, norm_gain_ref),
        (adapter_hbm, adapter_ref),
        (gate_hbm, gate),
        (down_hbm, down_table),
        (up_hbm, up_table),
    ]
    loads = [
        pltpu.make_async_copy(source, target, load_sem.at[i])
        for i, (source, target) in enumerate(copies)
    ]
    for load in loads[:later]:
        load.start()

    peers = [(dh, dr) for dh in range(head_count) for dr in range(rep_count)][1:]

    def peer_id(dh, dr):
        return {
            "head": lax.rem(head + dh, head_count),
            "rep": lax.rem(rep + dr, rep_count),
        }

    barrier = pltpu.get_barrier_semaphore()
    for dh, dr in peers:
        pl.semaphore_signal(barrier, inc=1, device_id=peer_id(dh, dr), device_id_type=MESH)

    @pl.when(ctx > 0)
    def _():
        pl.semaphore_signal(barrier, inc=1, device_id={"ctx": ctx - 1}, device_id_type=MESH)

    @pl.when(ctx < ctx_count - 1)
    def _():
        pl.semaphore_signal(barrier, inc=1, device_id={"ctx": ctx + 1}, device_id_type=MESH)

    @pl.when(first)
    def _():
        halo_in[...] = jnp.zeros_like(halo_in)
        state_in[...] = jnp.zeros_like(state_in)

    square_all[0] = jnp.zeros_like(square_all[0])

    block_ends = [(b + 1) * BLOCK - 1 for b in range(blocks)]
    for load in loads[:3]:
        load.wait()
    step_size_in = step_ref[...] + column(step_bias_ref[...])
    step_size = jnp.maximum(step_size_in, 0.0) + jnp.log1p(jnp.exp(-jnp.abs(step_size_in)))
    log_decay = -step_size * column(rate_ref[...])
    row_of = lax.broadcasted_iota(jnp.int32, (BLOCK, BLOCK), 0)
    col_of = lax.broadcasted_iota(jnp.int32, (BLOCK, BLOCK), 1)
    upto = jnp.where(row_of <= col_of, 1.0, 0.0).astype(bf16)
    spread_row = lax.rem(lax.broadcasted_iota(jnp.int32, (2 * heads, chunk), 0), heads)
    spread_col = lax.broadcasted_iota(jnp.int32, (2 * heads, chunk), 1) // head_size

    def lanes_of(c, width):
        if isinstance(c, int):
            return slice(c * width, (c + 1) * width)
        return pl.ds(pl.multiple_of(c * width, width), width)

    def widen(value, c):
        spread = jnp.where(spread_row == spread_col + c * (chunk // head_size), 1.0, 0.0)
        return lax.dot_general(
            value, spread.astype(bf16), (((0,), (0,)), ((), ())), preferred_element_type=f32
        )

    for b in range(blocks):
        at = slice(b * BLOCK, (b + 1) * BLOCK)
        sums = jnp.dot(split(log_decay[:, at], 3), upto, preferred_element_type=f32)
        cumulative = sums[:heads] + sums[heads : 2 * heads] + sums[2 * heads :]
        wide_ref[b, 0] = split(jnp.exp(cumulative), 2)
        wide_ref[b, 1] = split(jnp.exp(-cumulative) * step_size[:, at], 2)

    def open_wide(c):
        lanes = lanes_of(c, chunk)
        decay = 1.0
        for b in range(blocks):
            at = slice(b * BLOCK, (b + 1) * BLOCK)
            grown = widen(wide_ref[b, 0], c)
            grow[at, lanes] = grown
            local_y[at, lanes] = widen(wide_ref[b, 1], c)
            decay = decay * grown[BLOCK - 1 :]
        decay_ref[0:1, lanes] = decay

    for load in loads[3:6]:
        load.wait()
    top = lax.broadcasted_iota(jnp.int32, (EDGE, segment), 0) < EDGE // 2
    turn = lambda value: pltpu.roll(value, EDGE // 2, 0)
    ends = [tail_x[:, i * segment : (i + 1) * segment].astype(f32)[HALO - EDGE :] for i in range(4)]
    halo_out[:, :segment] = jnp.concatenate(
        [jnp.where(top, turn(ends[i]), ends[i + 1]) for i in (0, 2)], axis=0
    ).astype(bf16)
    here = coupling[...].astype(f32)
    for i in range(2):
        pad_bc[EDGE:, i * n : (i + 1) * n] = here[:, i]
    end_b, end_c = pad_bc[rows:, :n], pad_bc[rows:, n:]
    packed = jnp.where(top[:, :n], turn(end_b), end_c)
    halo_out[:, segment:] = jnp.concatenate([packed, packed], axis=0).astype(bf16)

    def conv_one(i, b):
        total = 0.0
        for k in range(taps):
            shift = EDGE - taps + 1 + k + b * BLOCK
            total = total + coupling_taps_ref[k, i : i + 1, :] * (
                pad_bc[shift : shift + BLOCK, i * n : (i + 1) * n]
            )
        return silu(total)

    def open_b(b):
        value = conv_one(0, b)
        b_keep[b] = value.astype(bf16)
        b_turned[b] = value.T.astype(bf16)

    def open_c(b):
        value = conv_one(1, b).astype(bf16)
        scores = lax.dot_general(
            value, b_keep[b], (((1,), (1,)), ((), ())), preferred_element_type=f32
        )
        lhs[b, :, :BLOCK] = jnp.where(row_of >= col_of, scores, 0.0).astype(bf16)
        lhs[b, :, BLOCK:] = value

    def unpack():
        value = halo_in[:, segment:].astype(f32)[:EDGE]
        pad_bc[:EDGE, :n] = turn(value)
        pad_bc[:EDGE, n:] = value
        for i in (0, 2):
            value = halo_in[:, :segment].astype(f32)[i // 2 * EDGE : (i // 2 + 1) * EDGE]
            pad_x[:EDGE, i * segment : (i + 1) * segment] = turn(value)
            pad_x[:EDGE, (i + 1) * segment : (i + 2) * segment] = value

    neighbours = jnp.minimum(ctx, 1) + jnp.minimum(ctx_count - 1 - ctx, 1)
    pl.semaphore_wait(barrier, len(peers) + neighbours)

    halo = pltpu.make_async_remote_copy(
        src_ref=halo_out,
        dst_ref=halo_in,
        send_sem=halo_send,
        recv_sem=halo_recv,
        device_id={"ctx": lax.rem(ctx + 1, ctx_count)},
        device_id_type=MESH,
    )

    @pl.when(ctx < ctx_count - 1)
    def _():
        halo.start()

    def load_rest():
        for load in loads[later:]:
            load.start()

    load_rest()
    for b in range(1, blocks):
        open_b(b)

    def parts(c):
        return [c * (chunk // BLOCK) + i for i in range(chunk // BLOCK)]

    def state_copy(c):
        return pltpu.make_async_remote_copy(
            src_ref=state_out.at[c],
            dst_ref=state_in.at[c],
            send_sem=state_send.at[c],
            recv_sem=state_recv.at[c],
            device_id={"ctx": lax.rem(ctx + 1, ctx_count)},
            device_id_type=MESH,
        )

    def loop(count, body):
        for c in range(count):
            body(c)

    def conv_signal(start, stop, lanes):
        total = 0.0
        for k in range(taps):
            shift = EDGE - taps + 1 + k + start
            total = total + signal_taps_ref[k : k + 1, lanes] * (
                pad_x[shift : shift + stop - start, lanes]
            )
        x_here = silu(total)
        conv_x[start:stop, lanes] = x_here.astype(bf16)
        b = start // BLOCK
        scaled = (x_here * local_y[start:stop, lanes]).astype(bf16)
        rhs[b, start - b * BLOCK : stop - b * BLOCK, lanes] = scaled
        return scaled

    def inside(c):
        lanes = lanes_of(c, chunk)
        loads[signal_at + c].wait()
        open_wide(c)
        pad_x[EDGE:, lanes] = signal[:, lanes].astype(f32)
        for b in range(1, blocks):
            scaled = conv_signal(b * BLOCK, (b + 1) * BLOCK, lanes)
            piece_ref[b - 1, :, lanes] = jnp.dot(b_turned[b], scaled, preferred_element_type=f32)
        conv_signal(HALO, BLOCK, lanes)

    def ahead(c):
        lanes = lanes_of(c, chunk)
        conv_signal(0, HALO, lanes)
        state = jnp.dot(b_turned[0], rhs[0, :BLOCK, lanes], preferred_element_type=f32)
        state = state * grow[block_ends[0] : block_ends[0] + 1, lanes]
        for b in range(1, blocks):
            rhs[b, BLOCK:, lanes] = state.astype(bf16)
            state = (state + piece_ref[b - 1, :, lanes]) * (
                grow[block_ends[b] : block_ends[b] + 1, lanes]
            )
        final[:, lanes] = state

    def send_own(p):
        state_out[p] = final[:, lanes_of(p, BLOCK)].astype(bf16)
        state_copy(p).start()

    loads[6].wait()

    @pl.when(first)
    def _():
        unpack()
        open_b(0)

        def step(c):
            inside(c)
            ahead(c)

            for p in parts(c):
                send_own(p)

        loop(chunks, step)

    @pl.when(ctx > 0)
    def _():
        loop(chunks, inside)

    for b in range(1, blocks):
        open_c(b)
    for load in loads[later + 2 : later + 3] + loads[later + 4 :]:
        load.wait()
    adapter = adapter_ref[0]
    held = down_table.shape[0]
    table_row = lax.rem(adapter, held)
    holder = adapter // held
    tables = []
    for i, (table, out, into) in enumerate(
        ((down_table, down_out, down_in), (up_table, up_out, up_in))
    ):
        width = out.shape[2]
        for dr in range(1, rep_count):
            other = lax.rem(rep + dr, rep_count)
            out[dr - 1] = table[table_row, :, pl.ds(pl.multiple_of(other * width, width), width)]
            copy = pltpu.make_async_remote_copy(
                src_ref=out.at[dr - 1],
                dst_ref=into.at[dr - 1],
                send_sem=table_send.at[i, dr - 1],
                recv_sem=table_recv.at[i, dr - 1],
                device_id={"rep": other},
                device_id_type=MESH,
            )
            copy.start()
            tables.append(copy)

    @pl.when(ctx > 0)
    def _():
        halo.wait_recv()
        unpack()
        open_b(0)
        loop(chunks, ahead)

    open_c(0)
    for i in (0, 1, 3):
        loads[later + i].wait()
    skip = lax.dot_general(
        split(jnp.broadcast_to(column(skip_ref[...]), (heads, EDGE)), 2),
        jnp.where(
            lax.rem(lax.broadcasted_iota(jnp.int32, (2 * heads, channels), 0), heads)
            == lax.broadcasted_iota(jnp.int32, (2 * heads, channels), 1) // head_size,
            1.0,
            0.0,
        ).astype(bf16),
        (((0,), (0,)), ((), ())),
        preferred_element_type=f32,
    )[:1]

    def forward(p):
        lanes = lanes_of(p, BLOCK)
        state_out[p] = (
            decay_ref[0:1, lanes] * state_in[p].astype(f32) + final[:, lanes]
        ).astype(bf16)
        state_copy(p).start()

    between = jnp.logical_and(ctx > 0, ctx < ctx_count - 1)
    for c in range(chunks):
        lanes = slice(c * chunk, (c + 1) * chunk)

        @pl.when(between)
        def _():
            for p in parts(c):
                state_copy(p).wait_recv()
                forward(p)

        decay = None
        for b in range(blocks):
            at = slice(b * BLOCK, (b + 1) * BLOCK)
            if b == 0:
                inner = jnp.dot(lhs[b, :, :BLOCK], rhs[b, :BLOCK, lanes], preferred_element_type=f32)
            else:
                inner = jnp.dot(lhs[b], rhs[b, :, lanes], preferred_element_type=f32)
            opened = silu(gate[at, lanes].astype(f32))
            growth = grow[at, lanes]
            y = growth * inner + skip[:, lanes] * conv_x[at, lanes].astype(f32)
            local_y[at, lanes] = y * opened
            end = growth[BLOCK - 1 :]
            spread_growth = growth * opened
            grow[at, lanes] = spread_growth if decay is None else spread_growth * decay
            decay = end if decay is None else decay * end

    for copy in tables:
        copy.wait_recv()

    def chosen(table, into):
        width = into.shape[-1]
        own = table[table_row, :, pl.ds(pl.multiple_of(rep * width, width), width)]
        value = own
        for dr in range(1, rep_count):
            source = lax.rem(rep - dr + rep_count, rep_count)
            here = jnp.full(own.shape, (holder == source).astype(jnp.int32), jnp.int32) > 0
            value = jnp.where(here, into[dr - 1].astype(f32), value.astype(f32)).astype(bf16)
        return value

    down_mine[...] = chosen(down_table, down_in)

    squares = [0.0] * blocks
    low = [0.0] * blocks
    for c in range(chunks):
        lanes = slice(c * chunk, (c + 1) * chunk)

        @pl.when(jnp.logical_and(last, ctx > 0))
        def _():
            for p in parts(c):
                state_copy(p).wait_recv()

        incoming = jnp.concatenate([state_in[p] for p in parts(c)], axis=1)
        for b in range(blocks):
            at = slice(b * BLOCK, (b + 1) * BLOCK)
            carried = jnp.dot(lhs[b, :, BLOCK:], incoming, preferred_element_type=f32)
            gated = local_y[at, lanes] + grow[at, lanes] * carried
            local_y[at, lanes] = gated
            square = gated * gated
            for piece in range(0, chunk, BLOCK):
                squares[b] = squares[b] + square[:, piece : piece + BLOCK]
            gained = (gated * norm_gain_ref[:, lanes]).astype(bf16)
            low[b] = low[b] + lax.dot_general(
                gained, down_mine[:, lanes], (((1,), (1,)), ((), ())), preferred_element_type=f32
            )
    low_own = jnp.concatenate(low, axis=0)
    half = rows // 2
    low_all[0] = jnp.concatenate([low_own[:half], low_own[half:]], axis=1).astype(bf16)
    ones = jnp.ones((EDGE, BLOCK), bf16)
    for b in range(blocks):
        terms = split(squares[b], 2)
        total = lax.dot_general(
            ones, terms, (((1,), (1,)), ((), ())), preferred_element_type=f32
        )
        square_all[0, b : b + 1] = total[:1, :BLOCK] + total[:1, BLOCK:]

    def exchange(slot, dh, dr):
        return [
            pltpu.make_async_remote_copy(
                src_ref=buffer.at[0],
                dst_ref=buffer.at[slot],
                send_sem=send.at[slot],
                recv_sem=recv.at[slot],
                device_id=peer_id(dh, dr),
                device_id_type=MESH,
            )
            for buffer, send, recv in (
                (square_all, square_send, square_recv),
                (low_all, low_send, low_recv),
            )
        ]

    exchanges = [exchange(slot + 1, dh, dr) for slot, (dh, dr) in enumerate(peers)]
    for square_copy, low_copy in exchanges:
        square_copy.start()
    for square_copy, low_copy in exchanges:
        low_copy.start()

    up_mine[...] = chosen(up_table, up_in)

    def inverse_of(dh):
        total = 0.0
        for dr in range(rep_count):
            total = total + square_all[dh * rep_count + dr]
        value = lax.rsqrt(total / (channels * rep_count) + epsilon)
        value = split(value, 3)
        out = []
        for b in range(blocks):
            mine = lax.broadcasted_iota(jnp.int32, value.shape[:1] + (BLOCK,), 0)
            mine = jnp.where(lax.rem(mine, total.shape[0]) == b, 1.0, 0.0).astype(bf16)
            out.append(
                lax.dot_general(
                    value, mine, (((0,), (0,)), ((), ())), preferred_element_type=f32
                )
            )
        return out

    for slot, (dh, dr) in enumerate(peers):
        if dh == 0:
            exchanges[slot][0].wait_recv()
    own_inverse = inverse_of(0)
    for c in range(channels // BLOCK):
        lanes = slice(c * BLOCK, (c + 1) * BLOCK)
        for b in range(blocks):
            at = slice(b * BLOCK, (b + 1) * BLOCK)
            mixer_ref[at, lanes] = (
                local_y[at, lanes] * own_inverse[b] * norm_gain_ref[:, lanes]
            ).astype(bf16)

    for slot, (dh, dr) in enumerate(peers):
        if dh > 0:
            exchanges[slot][0].wait_recv()
        exchanges[slot][1].wait_recv()
    reduced = 0.0
    for dh in range(head_count):
        inverse = own_inverse if dh == 0 else inverse_of(dh)
        inverse = jnp.concatenate(inverse, axis=0)[:, :rank]
        packed = 0.0
        for dr in range(rep_count):
            packed = packed + low_all[dh * rep_count + dr].astype(f32)
        reduced = reduced + inverse * jnp.concatenate([packed[:, :rank], packed[:, rank:]], axis=0)
    reduced_ref[...] = reduced.astype(bf16)

    for copy in tables:
        copy.wait_send()
    for pair in exchanges:
        for copy in pair:
            copy.wait_send()

    @pl.when(ctx < ctx_count - 1)
    def _():
        halo.wait_send()
        for p in range(channels // BLOCK):
            state_copy(p).wait_send()


def finish(mixer_ref, reduced_ref, up_ref, mixer_hbm, delta_hbm, delta, sem):
    rows, width = delta.shape
    mixer_copy = pltpu.make_async_copy(mixer_ref, mixer_hbm, sem.at[0])
    mixer_copy.start()
    step = width // PARTS
    copies = [mixer_copy]
    reduced = reduced_ref[...]
    for c in range(PARTS):
        lanes = pl.ds(c * step, step)
        delta[:, lanes] = jnp.dot(
            reduced, up_ref[:, lanes], preferred_element_type=jnp.float32
        ).astype(jnp.bfloat16)
        copy = pltpu.make_async_copy(delta.at[:, lanes], delta_hbm.at[:, lanes], sem.at[c + 1])
        copy.start()
        copies.append(copy)
    for copy in copies:
        copy.wait()


def local(
    axis_sizes,
    signal_input,
    gate_input,
    coupling_input,
    step_input,
    signal_taps,
    coupling_taps,
    step_bias,
    head_decay_rate,
    head_skip_gain,
    gated_norm_gain,
    request_adapter,
    stored_down_weight,
    stored_up_weight,
):
    ctx_count, head_count, rep_count = axis_sizes
    rows, channels = signal_input.shape
    n = coupling_input.shape[2]
    heads = step_input.shape[0]
    held, rank, down_width = stored_down_weight.shape
    up_width = stored_up_weight.shape[2] // rep_count
    chunk = 256
    pieces = channels // BLOCK
    blocks = rows // BLOCK
    devices = head_count * rep_count
    f32, bf16 = jnp.float32, jnp.bfloat16
    vmem = pl.BlockSpec(memory_space=pltpu.VMEM)
    hbm = pl.BlockSpec(memory_space=pltpu.HBM)
    dma = pltpu.SemaphoreType.DMA
    mixed, reduced, up_mine = pl.pallas_call(
        functools.partial(kernel, (ctx_count, head_count, rep_count, chunk)),
        out_shape=(
            pltpu.VMEM((rows, channels), bf16),
            pltpu.VMEM((rows, rank), bf16),
            pltpu.VMEM((rank, up_width), bf16),
        ),
        in_specs=[hbm] * 13,
        out_specs=(vmem, vmem, vmem),
        scratch_shapes=[
            pltpu.VMEM((rows, channels), bf16),
            pltpu.VMEM((rows, channels), bf16),
            pltpu.VMEM((rows, 2, n), bf16),
            pltpu.VMEM(stored_down_weight.shape, bf16),
            pltpu.VMEM(stored_up_weight.shape, bf16),
            pltpu.VMEM((HALO, channels), bf16),
            pltpu.VMEM((HALO, channels // 4 + n), bf16),
            pltpu.VMEM((HALO, channels // 4 + n), bf16),
            pltpu.VMEM((EDGE + rows, channels), f32),
            pltpu.VMEM((EDGE + rows, 2 * n), f32),
            pltpu.VMEM((rows, channels), bf16),
            pltpu.VMEM((blocks, BLOCK + n, channels), bf16),
            pltpu.VMEM((blocks, BLOCK, BLOCK + n), bf16),
            pltpu.VMEM((blocks, n, BLOCK), bf16),
            pltpu.VMEM((rows, channels), f32),
            pltpu.VMEM((rows, channels), f32),
            pltpu.VMEM((n, channels), f32),
            pltpu.VMEM((max(blocks - 1, 1), n, channels), f32),
            pltpu.VMEM((blocks, BLOCK, n), bf16),
            pltpu.VMEM((blocks, 2, 2 * heads, BLOCK), bf16),
            pltpu.VMEM((8, channels), f32),
            pltpu.SMEM((1,), jnp.int32),
            pltpu.VMEM((pieces, n, BLOCK), bf16),
            pltpu.VMEM((pieces, n, BLOCK), bf16),
            pltpu.VMEM((rep_count - 1, rank, channels), bf16),
            pltpu.VMEM((rep_count - 1, rank, channels), bf16),
            pltpu.VMEM((rank, channels), bf16),
            pltpu.VMEM((rep_count - 1, rank, up_width), bf16),
            pltpu.VMEM((rep_count - 1, rank, up_width), bf16),
            pltpu.VMEM((devices, rows // 2, 2 * rank), bf16),
            pltpu.VMEM((devices, -(-blocks // EDGE) * EDGE, BLOCK), f32),
            pltpu.VMEM(step_input.shape, f32),
            pltpu.VMEM(signal_taps.shape, f32),
            pltpu.VMEM(coupling_taps.shape, f32),
            pltpu.VMEM((1, heads), f32),
            pltpu.VMEM((1, heads), f32),
            pltpu.VMEM((1, heads), f32),
            pltpu.VMEM((1, channels), f32),
            dma((13 + channels // chunk,)),
            dma,
            dma,
            dma((2, rep_count - 1)),
            dma((2, rep_count - 1)),
            dma((pieces,)),
            dma((pieces,)),
            dma((devices,)),
            dma((devices,)),
            dma((devices,)),
            dma((devices,)),
        ],
        compiler_params=pltpu.CompilerParams(
            collective_id=0, has_side_effects=True, vmem_limit_bytes=62500000
        ),
    )(
        request_adapter,
        signal_input,
        gate_input,
        coupling_input,
        stored_down_weight,
        stored_up_weight,
        step_input,
        signal_taps,
        coupling_taps,
        step_bias.reshape(1, -1),
        head_decay_rate.reshape(1, -1),
        head_skip_gain.reshape(1, -1),
        gated_norm_gain.reshape(1, -1),
    )
    return pl.pallas_call(
        finish,
        out_shape=(
            jax.ShapeDtypeStruct((rows, channels), bf16),
            jax.ShapeDtypeStruct((rows, up_width), bf16),
        ),
        in_specs=[vmem, vmem, vmem],
        out_specs=(hbm, hbm),
        scratch_shapes=[pltpu.VMEM((rows, up_width), bf16), dma((PARTS + 1,))],
        compiler_params=pltpu.CompilerParams(vmem_limit_bytes=8000000),
    )(mixed, reduced, up_mine)


def solution(mesh):
    in_specs = (
        P(("group", "ctx"), ("head", "rep")),
        P(("group", "ctx"), ("head", "rep")),
        P(("group", "ctx"), None, "head"),
        P(("head", "rep"), ("group", "ctx")),
        P(None, ("head", "rep")),
        P(None, None, "head"),
        P(("head", "rep")),
        P(("head", "rep")),
        P(("head", "rep")),
        P(("head", "rep")),
        P("group"),
        P("rep", None, "head"),
        P("rep", None, "head"),
    )
    out_specs = (P(("group", "ctx"), ("head", "rep")), P(("group", "ctx"), ("head", "rep")))
    axis_sizes = tuple(mesh.shape[name] for name in ("ctx", "head", "rep"))
    return jax.shard_map(
        functools.partial(local, axis_sizes),
        mesh=mesh,
        in_specs=in_specs,
        out_specs=out_specs,
        check_vma=False,
    )
```

```python
import functools

import jax
import jax.numpy as jnp
from jax import lax
from jax.experimental import pallas as pl
from jax.experimental.pallas import tpu as pltpu
from jax.sharding import PartitionSpec as P

BLOCK = 128
MESH = pl.DeviceIdType.MESH
HALO = 16
PARTS = 4
EARLY = 2
EDGE = 8
epsilon = 1e-05


def silu(value):
    half = 0.5 * value
    return half * jnp.tanh(half) + half


def split(value, terms):
    parts = []
    for _ in range(terms):
        top = value.astype(jnp.bfloat16)
        parts.append(top)
        value = value - top.astype(jnp.float32)
    return jnp.concatenate(parts, axis=0)


def column(row):
    size = row.shape[1]
    eye = lax.broadcasted_iota(jnp.int32, (size, size), 0) == lax.broadcasted_iota(
        jnp.int32, (size, size), 1
    )
    spread = jnp.broadcast_to(row, (size, size))
    return jnp.sum(jnp.where(eye, spread, 0.0), axis=1, keepdims=True)


def kernel(
    sizes,
    adapter_hbm,
    signal_hbm,
    gate_hbm,
    coupling_hbm,
    down_hbm,
    up_hbm,
    step_hbm,
    signal_taps_hbm,
    coupling_taps_hbm,
    step_bias_hbm,
    rate_hbm,
    skip_hbm,
    norm_gain_hbm,
    mixer_ref,
    reduced_ref,
    up_mine,
    signal,
    gate,
    coupling,
    down_table,
    up_table,
    tail_x,
    halo_out,
    halo_in,
    pad_x,
    pad_bc,
    conv_x,
    rhs,
    lhs,
    b_turned,
    grow,
    local_y,
    final,
    piece_ref,
    b_keep,
    wide_ref,
    decay_ref,
    adapter_ref,
    state_out,
    state_in,
    down_out,
    down_in,
    down_mine,
    up_out,
    up_in,
    low_all,
    square_all,
    step_ref,
    signal_taps_ref,
    coupling_taps_ref,
    step_bias_ref,
    rate_ref,
    skip_ref,
    norm_gain_ref,
    load_sem,
    halo_send,
    halo_recv,
    table_send,
    table_recv,
    state_send,
    state_recv,
    low_send,
    low_recv,
    square_send,
    square_recv,
):
    ctx_count, head_count, rep_count, chunk = sizes
    ctx, head, rep = (lax.axis_index(name) for name in ("ctx", "head", "rep"))
    rows, channels = signal.shape
    heads = step_ref.shape[0]
    head_size = channels // heads
    n = coupling.shape[2]
    taps = signal_taps_ref.shape[0]
    blocks = rows // BLOCK
    chunks = channels // chunk
    rank = down_mine.shape[0]
    up_width = up_in.shape[2]
    first, last = ctx == 0, ctx == ctx_count - 1
    f32, bf16 = jnp.float32, jnp.bfloat16

    segment = channels // 4
    copies = [
        (step_hbm, step_ref),
        (step_bias_hbm, step_bias_ref),
        (rate_hbm, rate_ref),
        (coupling_hbm, coupling),
        (coupling_taps_hbm, coupling_taps_ref),
        (signal_hbm.at[pl.ds(rows - HALO, HALO)], tail_x),
        (signal_taps_hbm, signal_taps_ref),
    ]
    signal_at = len(copies)
    for c in range(chunks):
        lanes = pl.ds(c * chunk, chunk)
        copies.append((signal_hbm.at[:, lanes], signal.at[:, lanes]))
    later = len(copies)
    copies += [
        (skip_hbm, skip_ref),
        (norm_gain_hbm, norm_gain_ref),
        (adapter_hbm, adapter_ref),
        (gate_hbm, gate),
        (down_hbm, down_table),
        (up_hbm, up_table),
    ]
    loads = [
        pltpu.make_async_copy(source, target, load_sem.at[i])
        for i, (source, target) in enumerate(copies)
    ]
    for load in loads[:later]:
        load.start()

    peers = [(dh, dr) for dh in range(head_count) for dr in range(rep_count)][1:]

    def peer_id(dh, dr):
        return {
            "head": lax.rem(head + dh, head_count),
            "rep": lax.rem(rep + dr, rep_count),
        }

    barrier = pltpu.get_barrier_semaphore()
    for dh, dr in peers:
        pl.semaphore_signal(barrier, inc=1, device_id=peer_id(dh, dr), device_id_type=MESH)

    @pl.when(ctx > 0)
    def _():
        pl.semaphore_signal(barrier, inc=1, device_id={"ctx": ctx - 1}, device_id_type=MESH)

    @pl.when(ctx < ctx_count - 1)
    def _():
        pl.semaphore_signal(barrier, inc=1, device_id={"ctx": ctx + 1}, device_id_type=MESH)

    @pl.when(first)
    def _():
        halo_in[...] = jnp.zeros_like(halo_in)
        state_in[...] = jnp.zeros_like(state_in)

    square_all[0] = jnp.zeros_like(square_all[0])

    block_ends = [(b + 1) * BLOCK - 1 for b in range(blocks)]
    for load in loads[:3]:
        load.wait()
    step_size_in = step_ref[...] + column(step_bias_ref[...])
    step_size = jnp.maximum(step_size_in, 0.0) + jnp.log1p(jnp.exp(-jnp.abs(step_size_in)))
    log_decay = -step_size * column(rate_ref[...])
    row_of = lax.broadcasted_iota(jnp.int32, (BLOCK, BLOCK), 0)
    col_of = lax.broadcasted_iota(jnp.int32, (BLOCK, BLOCK), 1)
    upto = jnp.where(row_of <= col_of, 1.0, 0.0).astype(bf16)
    spread_row = lax.rem(lax.broadcasted_iota(jnp.int32, (2 * heads, chunk), 0), heads)
    spread_col = lax.broadcasted_iota(jnp.int32, (2 * heads, chunk), 1) // head_size

    def lanes_of(c, width):
        if isinstance(c, int):
            return slice(c * width, (c + 1) * width)
        return pl.ds(pl.multiple_of(c * width, width), width)

    def widen(value, c):
        spread = jnp.where(spread_row == spread_col + c * (chunk // head_size), 1.0, 0.0)
        return lax.dot_general(
            value, spread.astype(bf16), (((0,), (0,)), ((), ())), preferred_element_type=f32
        )

    for b in range(blocks):
        at = slice(b * BLOCK, (b + 1) * BLOCK)
        sums = jnp.dot(split(log_decay[:, at], 3), upto, preferred_element_type=f32)
        cumulative = sums[:heads] + sums[heads : 2 * heads] + sums[2 * heads :]
        wide_ref[b, 0] = split(jnp.exp(cumulative), 2)
        wide_ref[b, 1] = split(jnp.exp(-cumulative) * step_size[:, at], 2)

    def open_wide(c):
        lanes = lanes_of(c, chunk)
        decay = 1.0
        for b in range(blocks):
            at = slice(b * BLOCK, (b + 1) * BLOCK)
            grown = widen(wide_ref[b, 0], c)
            grow[at, lanes] = grown
            local_y[at, lanes] = widen(wide_ref[b, 1], c)
            decay = decay * grown[BLOCK - 1 :]
        decay_ref[0:1, lanes] = decay

    for load in loads[3:6]:
        load.wait()
    top = lax.broadcasted_iota(jnp.int32, (EDGE, segment), 0) < EDGE // 2
    turn = lambda value: pltpu.roll(value, EDGE // 2, 0)
    ends = [tail_x[:, i * segment : (i + 1) * segment].astype(f32)[HALO - EDGE :] for i in range(4)]
    halo_out[:, :segment] = jnp.concatenate(
        [jnp.where(top, turn(ends[i]), ends[i + 1]) for i in (0, 2)], axis=0
    ).astype(bf16)
    here = coupling[...].astype(f32)
    for i in range(2):
        pad_bc[EDGE:, i * n : (i + 1) * n] = here[:, i]
    end_b, end_c = pad_bc[rows:, :n], pad_bc[rows:, n:]
    packed = jnp.where(top[:, :n], turn(end_b), end_c)
    halo_out[:, segment:] = jnp.concatenate([packed, packed], axis=0).astype(bf16)

    def conv_one(i, b):
        total = 0.0
        for k in range(taps):
            shift = EDGE - taps + 1 + k + b * BLOCK
            total = total + coupling_taps_ref[k, i : i + 1, :] * (
                pad_bc[shift : shift + BLOCK, i * n : (i + 1) * n]
            )
        return silu(total)

    def open_b(b):
        value = conv_one(0, b)
        b_keep[b] = value.astype(bf16)
        b_turned[b] = value.T.astype(bf16)

    def open_c(b):
        value = conv_one(1, b).astype(bf16)
        scores = lax.dot_general(
            value, b_keep[b], (((1,), (1,)), ((), ())), preferred_element_type=f32
        )
        lhs[b, :, :BLOCK] = jnp.where(row_of >= col_of, scores, 0.0).astype(bf16)
        lhs[b, :, BLOCK:] = value

    def unpack():
        value = halo_in[:, segment:].astype(f32)[:EDGE]
        pad_bc[:EDGE, :n] = turn(value)
        pad_bc[:EDGE, n:] = value
        for i in (0, 2):
            value = halo_in[:, :segment].astype(f32)[i // 2 * EDGE : (i // 2 + 1) * EDGE]
            pad_x[:EDGE, i * segment : (i + 1) * segment] = turn(value)
            pad_x[:EDGE, (i + 1) * segment : (i + 2) * segment] = value

    for b in range(1, blocks):
        open_b(b)
    neighbours = jnp.minimum(ctx, 1) + jnp.minimum(ctx_count - 1 - ctx, 1)
    pl.semaphore_wait(barrier, len(peers) + neighbours)

    halo = pltpu.make_async_remote_copy(
        src_ref=halo_out,
        dst_ref=halo_in,
        send_sem=halo_send,
        recv_sem=halo_recv,
        device_id={"ctx": lax.rem(ctx + 1, ctx_count)},
        device_id_type=MESH,
    )

    @pl.when(ctx < ctx_count - 1)
    def _():
        halo.start()

    def load_rest():
        for load in loads[later:]:
            load.start()

    load_rest()

    def parts(c):
        return [c * (chunk // BLOCK) + i for i in range(chunk // BLOCK)]

    def state_copy(c):
        return pltpu.make_async_remote_copy(
            src_ref=state_out.at[c],
            dst_ref=state_in.at[c],
            send_sem=state_send.at[c],
            recv_sem=state_recv.at[c],
            device_id={"ctx": lax.rem(ctx + 1, ctx_count)},
            device_id_type=MESH,
        )

    def loop(count, body):
        for c in range(count):
            body(c)

    def conv_signal(start, stop, lanes):
        total = 0.0
        for k in range(taps):
            shift = EDGE - taps + 1 + k + start
            total = total + signal_taps_ref[k : k + 1, lanes] * (
                pad_x[shift : shift + stop - start, lanes]
            )
        x_here = silu(total)
        conv_x[start:stop, lanes] = x_here.astype(bf16)
        b = start // BLOCK
        scaled = (x_here * local_y[start:stop, lanes]).astype(bf16)
        rhs[b, start - b * BLOCK : stop - b * BLOCK, lanes] = scaled
        return scaled

    def inside(c):
        lanes = lanes_of(c, chunk)
        loads[signal_at + c].wait()
        open_wide(c)
        pad_x[EDGE:, lanes] = signal[:, lanes].astype(f32)
        for b in range(1, blocks):
            scaled = conv_signal(b * BLOCK, (b + 1) * BLOCK, lanes)
            piece_ref[b - 1, :, lanes] = jnp.dot(b_turned[b], scaled, preferred_element_type=f32)
        conv_signal(HALO, BLOCK, lanes)

    def ahead(c):
        lanes = lanes_of(c, chunk)
        conv_signal(0, HALO, lanes)
        state = jnp.dot(b_turned[0], rhs[0, :BLOCK, lanes], preferred_element_type=f32)
        state = state * grow[block_ends[0] : block_ends[0] + 1, lanes]
        for b in range(1, blocks):
            rhs[b, BLOCK:, lanes] = state.astype(bf16)
            state = (state + piece_ref[b - 1, :, lanes]) * (
                grow[block_ends[b] : block_ends[b] + 1, lanes]
            )
        final[:, lanes] = state

    def send_own(p):
        state_out[p] = final[:, lanes_of(p, BLOCK)].astype(bf16)
        state_copy(p).start()

    loads[6].wait()

    @pl.when(first)
    def _():
        unpack()
        open_b(0)

        def step(c):
            inside(c)
            ahead(c)

            for p in parts(c):
                send_own(p)

        loop(chunks, step)

    @pl.when(ctx > 0)
    def _():
        loop(chunks, inside)

    for b in range(1, blocks):
        open_c(b)
    for load in loads[later + 2 : later + 3] + loads[later + 4 :]:
        load.wait()
    adapter = adapter_ref[0]
    held = down_table.shape[0]
    table_row = lax.rem(adapter, held)
    holder = adapter // held
    tables = []
    for i, (table, out, into) in enumerate(
        ((down_table, down_out, down_in), (up_table, up_out, up_in))
    ):
        width = out.shape[2]
        for dr in range(1, rep_count):
            other = lax.rem(rep + dr, rep_count)
            out[dr - 1] = table[table_row, :, pl.ds(pl.multiple_of(other * width, width), width)]
            copy = pltpu.make_async_remote_copy(
                src_ref=out.at[dr - 1],
                dst_ref=into.at[dr - 1],
                send_sem=table_send.at[i, dr - 1],
                recv_sem=table_recv.at[i, dr - 1],
                device_id={"rep": other},
                device_id_type=MESH,
            )
            copy.start()
            tables.append(copy)

    def forward(p):
        lanes = lanes_of(p, BLOCK)
        state_out[p] = (
            decay_ref[0:1, lanes] * state_in[p].astype(f32) + final[:, lanes]
        ).astype(bf16)
        state_copy(p).start()

    between = jnp.logical_and(ctx > 0, ctx < ctx_count - 1)

    def pass_on(c):
        @pl.when(between)
        def _():
            for p in parts(c):
                state_copy(p).wait_recv()
                forward(p)

    early = min(EARLY, chunks)

    @pl.when(ctx > 0)
    def _():
        halo.wait_recv()
        unpack()
        open_b(0)
        done = 0
        for c in range(early):
            for a in range(done, min(chunks, 2 * c + 1)):
                ahead(a)
            done = max(done, min(chunks, 2 * c + 1))
            pass_on(c)
        for a in range(done, chunks):
            ahead(a)

    open_c(0)
    for i in (0, 1, 3):
        loads[later + i].wait()
    skip = lax.dot_general(
        split(jnp.broadcast_to(column(skip_ref[...]), (heads, EDGE)), 2),
        jnp.where(
            lax.rem(lax.broadcasted_iota(jnp.int32, (2 * heads, channels), 0), heads)
            == lax.broadcasted_iota(jnp.int32, (2 * heads, channels), 1) // head_size,
            1.0,
            0.0,
        ).astype(bf16),
        (((0,), (0,)), ((), ())),
        preferred_element_type=f32,
    )[:1]

    for c in range(chunks):
        lanes = slice(c * chunk, (c + 1) * chunk)

        if c + early < chunks:
            pass_on(c + early)

        decay = None
        for b in range(blocks):
            at = slice(b * BLOCK, (b + 1) * BLOCK)
            if b == 0:
                inner = jnp.dot(lhs[b, :, :BLOCK], rhs[b, :BLOCK, lanes], preferred_element_type=f32)
            else:
                inner = jnp.dot(lhs[b], rhs[b, :, lanes], preferred_element_type=f32)
            opened = silu(gate[at, lanes].astype(f32))
            growth = grow[at, lanes]
            y = growth * inner + skip[:, lanes] * conv_x[at, lanes].astype(f32)
            local_y[at, lanes] = y * opened
            end = growth[BLOCK - 1 :]
            spread_growth = growth * opened
            grow[at, lanes] = spread_growth if decay is None else spread_growth * decay
            decay = end if decay is None else decay * end

    for copy in tables:
        copy.wait_recv()

    def chosen(table, into):
        width = into.shape[-1]
        own = table[table_row, :, pl.ds(pl.multiple_of(rep * width, width), width)]
        value = own
        for dr in range(1, rep_count):
            source = lax.rem(rep - dr + rep_count, rep_count)
            here = jnp.full(own.shape, (holder == source).astype(jnp.int32), jnp.int32) > 0
            value = jnp.where(here, into[dr - 1].astype(f32), value.astype(f32)).astype(bf16)
        return value

    down_mine[...] = chosen(down_table, down_in)

    squares = [0.0] * blocks
    low = [0.0] * blocks
    for c in range(chunks):
        lanes = slice(c * chunk, (c + 1) * chunk)

        @pl.when(jnp.logical_and(last, ctx > 0))
        def _():
            for p in parts(c):
                state_copy(p).wait_recv()

        incoming = jnp.concatenate([state_in[p] for p in parts(c)], axis=1)
        for b in range(blocks):
            at = slice(b * BLOCK, (b + 1) * BLOCK)
            carried = jnp.dot(lhs[b, :, BLOCK:], incoming, preferred_element_type=f32)
            gated = local_y[at, lanes] + grow[at, lanes] * carried
            local_y[at, lanes] = gated
            square = gated * gated
            for piece in range(0, chunk, BLOCK):
                squares[b] = squares[b] + square[:, piece : piece + BLOCK]
            gained = (gated * norm_gain_ref[:, lanes]).astype(bf16)
            low[b] = low[b] + lax.dot_general(
                gained, down_mine[:, lanes], (((1,), (1,)), ((), ())), preferred_element_type=f32
            )
    low_own = jnp.concatenate(low, axis=0)
    half = rows // 2
    low_all[0] = jnp.concatenate([low_own[:half], low_own[half:]], axis=1).astype(bf16)
    ones = jnp.ones((EDGE, BLOCK), bf16)
    for b in range(blocks):
        terms = split(squares[b], 2)
        total = lax.dot_general(
            ones, terms, (((1,), (1,)), ((), ())), preferred_element_type=f32
        )
        square_all[0, b : b + 1] = total[:1, :BLOCK] + total[:1, BLOCK:]

    def exchange(slot, dh, dr):
        return [
            pltpu.make_async_remote_copy(
                src_ref=buffer.at[0],
                dst_ref=buffer.at[slot],
                send_sem=send.at[slot],
                recv_sem=recv.at[slot],
                device_id=peer_id(dh, dr),
                device_id_type=MESH,
            )
            for buffer, send, recv in (
                (square_all, square_send, square_recv),
                (low_all, low_send, low_recv),
            )
        ]

    exchanges = [exchange(slot + 1, dh, dr) for slot, (dh, dr) in enumerate(peers)]
    for square_copy, low_copy in exchanges:
        square_copy.start()
    for square_copy, low_copy in exchanges:
        low_copy.start()

    up_mine[...] = chosen(up_table, up_in)

    def inverse_of(dh):
        total = 0.0
        for dr in range(rep_count):
            total = total + square_all[dh * rep_count + dr]
        value = lax.rsqrt(total / (channels * rep_count) + epsilon)
        value = split(value, 3)
        out = []
        for b in range(blocks):
            mine = lax.broadcasted_iota(jnp.int32, value.shape[:1] + (BLOCK,), 0)
            mine = jnp.where(lax.rem(mine, total.shape[0]) == b, 1.0, 0.0).astype(bf16)
            out.append(
                lax.dot_general(
                    value, mine, (((0,), (0,)), ((), ())), preferred_element_type=f32
                )
            )
        return out

    for slot, (dh, dr) in enumerate(peers):
        if dh == 0:
            exchanges[slot][0].wait_recv()
    own_inverse = inverse_of(0)
    for c in range(channels // BLOCK):
        lanes = slice(c * BLOCK, (c + 1) * BLOCK)
        for b in range(blocks):
            at = slice(b * BLOCK, (b + 1) * BLOCK)
            mixer_ref[at, lanes] = (
                local_y[at, lanes] * own_inverse[b] * norm_gain_ref[:, lanes]
            ).astype(bf16)

    for slot, (dh, dr) in enumerate(peers):
        if dh > 0:
            exchanges[slot][0].wait_recv()
        exchanges[slot][1].wait_recv()
    reduced = 0.0
    for dh in range(head_count):
        inverse = own_inverse if dh == 0 else inverse_of(dh)
        inverse = jnp.concatenate(inverse, axis=0)[:, :rank]
        packed = 0.0
        for dr in range(rep_count):
            packed = packed + low_all[dh * rep_count + dr].astype(f32)
        reduced = reduced + inverse * jnp.concatenate([packed[:, :rank], packed[:, rank:]], axis=0)
    reduced_ref[...] = reduced.astype(bf16)

    for copy in tables:
        copy.wait_send()
    for pair in exchanges:
        for copy in pair:
            copy.wait_send()

    @pl.when(ctx < ctx_count - 1)
    def _():
        halo.wait_send()
        for p in range(channels // BLOCK):
            state_copy(p).wait_send()


def finish(mixer_ref, reduced_ref, up_ref, mixer_hbm, delta_hbm, delta, sem):
    rows, width = delta.shape
    mixer_copy = pltpu.make_async_copy(mixer_ref, mixer_hbm, sem.at[0])
    mixer_copy.start()
    step = width // PARTS
    copies = [mixer_copy]
    reduced = reduced_ref[...]
    for c in range(PARTS):
        lanes = pl.ds(c * step, step)
        delta[:, lanes] = jnp.dot(
            reduced, up_ref[:, lanes], preferred_element_type=jnp.float32
        ).astype(jnp.bfloat16)
        copy = pltpu.make_async_copy(delta.at[:, lanes], delta_hbm.at[:, lanes], sem.at[c + 1])
        copy.start()
        copies.append(copy)
    for copy in copies:
        copy.wait()


def local(
    axis_sizes,
    signal_input,
    gate_input,
    coupling_input,
    step_input,
    signal_taps,
    coupling_taps,
    step_bias,
    head_decay_rate,
    head_skip_gain,
    gated_norm_gain,
    request_adapter,
    stored_down_weight,
    stored_up_weight,
):
    ctx_count, head_count, rep_count = axis_sizes
    rows, channels = signal_input.shape
    n = coupling_input.shape[2]
    heads = step_input.shape[0]
    held, rank, down_width = stored_down_weight.shape
    up_width = stored_up_weight.shape[2] // rep_count
    chunk = 256
    pieces = channels // BLOCK
    blocks = rows // BLOCK
    devices = head_count * rep_count
    f32, bf16 = jnp.float32, jnp.bfloat16
    vmem = pl.BlockSpec(memory_space=pltpu.VMEM)
    hbm = pl.BlockSpec(memory_space=pltpu.HBM)
    dma = pltpu.SemaphoreType.DMA
    mixed, reduced, up_mine = pl.pallas_call(
        functools.partial(kernel, (ctx_count, head_count, rep_count, chunk)),
        out_shape=(
            pltpu.VMEM((rows, channels), bf16),
            pltpu.VMEM((rows, rank), bf16),
            pltpu.VMEM((rank, up_width), bf16),
        ),
        in_specs=[hbm] * 13,
        out_specs=(vmem, vmem, vmem),
        scratch_shapes=[
            pltpu.VMEM((rows, channels), bf16),
            pltpu.VMEM((rows, channels), bf16),
            pltpu.VMEM((rows, 2, n), bf16),
            pltpu.VMEM(stored_down_weight.shape, bf16),
            pltpu.VMEM(stored_up_weight.shape, bf16),
            pltpu.VMEM((HALO, channels), bf16),
            pltpu.VMEM((HALO, channels // 4 + n), bf16),
            pltpu.VMEM((HALO, channels // 4 + n), bf16),
            pltpu.VMEM((EDGE + rows, channels), f32),
            pltpu.VMEM((EDGE + rows, 2 * n), f32),
            pltpu.VMEM((rows, channels), bf16),
            pltpu.VMEM((blocks, BLOCK + n, channels), bf16),
            pltpu.VMEM((blocks, BLOCK, BLOCK + n), bf16),
            pltpu.VMEM((blocks, n, BLOCK), bf16),
            pltpu.VMEM((rows, channels), f32),
            pltpu.VMEM((rows, channels), f32),
            pltpu.VMEM((n, channels), f32),
            pltpu.VMEM((max(blocks - 1, 1), n, channels), f32),
            pltpu.VMEM((blocks, BLOCK, n), bf16),
            pltpu.VMEM((blocks, 2, 2 * heads, BLOCK), bf16),
            pltpu.VMEM((8, channels), f32),
            pltpu.SMEM((1,), jnp.int32),
            pltpu.VMEM((pieces, n, BLOCK), bf16),
            pltpu.VMEM((pieces, n, BLOCK), bf16),
            pltpu.VMEM((rep_count - 1, rank, channels), bf16),
            pltpu.VMEM((rep_count - 1, rank, channels), bf16),
            pltpu.VMEM((rank, channels), bf16),
            pltpu.VMEM((rep_count - 1, rank, up_width), bf16),
            pltpu.VMEM((rep_count - 1, rank, up_width), bf16),
            pltpu.VMEM((devices, rows // 2, 2 * rank), bf16),
            pltpu.VMEM((devices, -(-blocks // EDGE) * EDGE, BLOCK), f32),
            pltpu.VMEM(step_input.shape, f32),
            pltpu.VMEM(signal_taps.shape, f32),
            pltpu.VMEM(coupling_taps.shape, f32),
            pltpu.VMEM((1, heads), f32),
            pltpu.VMEM((1, heads), f32),
            pltpu.VMEM((1, heads), f32),
            pltpu.VMEM((1, channels), f32),
            dma((13 + channels // chunk,)),
            dma,
            dma,
            dma((2, rep_count - 1)),
            dma((2, rep_count - 1)),
            dma((pieces,)),
            dma((pieces,)),
            dma((devices,)),
            dma((devices,)),
            dma((devices,)),
            dma((devices,)),
        ],
        compiler_params=pltpu.CompilerParams(
            collective_id=0, has_side_effects=True, vmem_limit_bytes=62500000
        ),
    )(
        request_adapter,
        signal_input,
        gate_input,
        coupling_input,
        stored_down_weight,
        stored_up_weight,
        step_input,
        signal_taps,
        coupling_taps,
        step_bias.reshape(1, -1),
        head_decay_rate.reshape(1, -1),
        head_skip_gain.reshape(1, -1),
        gated_norm_gain.reshape(1, -1),
    )
    return pl.pallas_call(
        finish,
        out_shape=(
            jax.ShapeDtypeStruct((rows, channels), bf16),
            jax.ShapeDtypeStruct((rows, up_width), bf16),
        ),
        in_specs=[vmem, vmem, vmem],
        out_specs=(hbm, hbm),
        scratch_shapes=[pltpu.VMEM((rows, up_width), bf16), dma((PARTS + 1,))],
        compiler_params=pltpu.CompilerParams(vmem_limit_bytes=8000000),
    )(mixed, reduced, up_mine)


def solution(mesh):
    in_specs = (
        P(("group", "ctx"), ("head", "rep")),
        P(("group", "ctx"), ("head", "rep")),
        P(("group", "ctx"), None, "head"),
        P(("head", "rep"), ("group", "ctx")),
        P(None, ("head", "rep")),
        P(None, None, "head"),
        P(("head", "rep")),
        P(("head", "rep")),
        P(("head", "rep")),
        P(("head", "rep")),
        P("group"),
        P("rep", None, "head"),
        P("rep", None, "head"),
    )
    out_specs = (P(("group", "ctx"), ("head", "rep")), P(("group", "ctx"), ("head", "rep")))
    axis_sizes = tuple(mesh.shape[name] for name in ("ctx", "head", "rep"))
    return jax.shard_map(
        functools.partial(local, axis_sizes),
        mesh=mesh,
        in_specs=in_specs,
        out_specs=out_specs,
        check_vma=False,
    )
```

```python
import functools

import jax
import jax.numpy as jnp
from jax import lax
from jax.experimental import pallas as pl
from jax.experimental.pallas import tpu as pltpu
from jax.sharding import PartitionSpec as P

BLOCK = 128
MESH = pl.DeviceIdType.MESH
HALO = 16
PARTS = 4
EARLY = 2
EDGE = 8
epsilon = 1e-05


def silu(value):
    half = 0.5 * value
    return half * jnp.tanh(half) + half


def split(value, terms):
    parts = []
    for _ in range(terms):
        top = value.astype(jnp.bfloat16)
        parts.append(top)
        value = value - top.astype(jnp.float32)
    return jnp.concatenate(parts, axis=0)


def column(row):
    size = row.shape[1]
    eye = lax.broadcasted_iota(jnp.int32, (size, size), 0) == lax.broadcasted_iota(
        jnp.int32, (size, size), 1
    )
    spread = jnp.broadcast_to(row, (size, size))
    return jnp.sum(jnp.where(eye, spread, 0.0), axis=1, keepdims=True)


def kernel(
    sizes,
    adapter_hbm,
    signal_hbm,
    gate_hbm,
    coupling_hbm,
    down_hbm,
    up_hbm,
    step_hbm,
    signal_taps_hbm,
    coupling_taps_hbm,
    step_bias_hbm,
    rate_hbm,
    skip_hbm,
    norm_gain_hbm,
    mixer_ref,
    reduced_ref,
    up_mine,
    signal,
    gate,
    coupling,
    down_table,
    up_table,
    tail_x,
    halo_out,
    halo_in,
    pad_x,
    pad_bc,
    conv_x,
    rhs,
    lhs,
    b_turned,
    grow,
    local_y,
    final,
    piece_ref,
    b_keep,
    wide_ref,
    decay_ref,
    adapter_ref,
    state_out,
    state_in,
    down_out,
    down_in,
    down_mine,
    up_out,
    up_in,
    low_all,
    square_all,
    step_ref,
    signal_taps_ref,
    coupling_taps_ref,
    step_bias_ref,
    rate_ref,
    skip_ref,
    norm_gain_ref,
    load_sem,
    halo_send,
    halo_recv,
    table_send,
    table_recv,
    state_send,
    state_recv,
    low_send,
    low_recv,
    square_send,
    square_recv,
):
    ctx_count, head_count, rep_count, chunk = sizes
    ctx, head, rep = (lax.axis_index(name) for name in ("ctx", "head", "rep"))
    rows, channels = signal.shape
    heads = step_ref.shape[0]
    head_size = channels // heads
    n = coupling.shape[2]
    taps = signal_taps_ref.shape[0]
    blocks = rows // BLOCK
    chunks = channels // chunk
    rank = down_mine.shape[0]
    up_width = up_in.shape[2]
    first, last = ctx == 0, ctx == ctx_count - 1
    f32, bf16 = jnp.float32, jnp.bfloat16

    segment = channels // 4
    copies = [
        (step_hbm, step_ref),
        (step_bias_hbm, step_bias_ref),
        (rate_hbm, rate_ref),
        (coupling_hbm, coupling),
        (coupling_taps_hbm, coupling_taps_ref),
        (signal_hbm.at[pl.ds(rows - HALO, HALO)], tail_x),
        (signal_taps_hbm, signal_taps_ref),
    ]
    signal_at = len(copies)
    for c in range(chunks):
        lanes = pl.ds(c * chunk, chunk)
        copies.append((signal_hbm.at[:, lanes], signal.at[:, lanes]))
    later = len(copies)
    copies += [
        (skip_hbm, skip_ref),
        (norm_gain_hbm, norm_gain_ref),
        (adapter_hbm, adapter_ref),
        (gate_hbm, gate),
        (down_hbm, down_table),
        (up_hbm, up_table),
    ]
    loads = [
        pltpu.make_async_copy(source, target, load_sem.at[i])
        for i, (source, target) in enumerate(copies)
    ]
    for load in loads[:later]:
        load.start()

    peers = [(dh, dr) for dh in range(head_count) for dr in range(rep_count)][1:]

    def peer_id(dh, dr):
        return {
            "head": lax.rem(head + dh, head_count),
            "rep": lax.rem(rep + dr, rep_count),
        }

    barrier = pltpu.get_barrier_semaphore()
    for dh, dr in peers:
        pl.semaphore_signal(barrier, inc=1, device_id=peer_id(dh, dr), device_id_type=MESH)

    @pl.when(ctx > 0)
    def _():
        pl.semaphore_signal(barrier, inc=1, device_id={"ctx": ctx - 1}, device_id_type=MESH)

    @pl.when(ctx < ctx_count - 1)
    def _():
        pl.semaphore_signal(barrier, inc=1, device_id={"ctx": ctx + 1}, device_id_type=MESH)

    @pl.when(first)
    def _():
        halo_in[...] = jnp.zeros_like(halo_in)
        state_in[...] = jnp.zeros_like(state_in)

    square_all[0] = jnp.zeros_like(square_all[0])

    block_ends = [(b + 1) * BLOCK - 1 for b in range(blocks)]
    for load in loads[:3]:
        load.wait()
    step_size_in = step_ref[...] + column(step_bias_ref[...])
    step_size = jnp.maximum(step_size_in, 0.0) + jnp.log1p(jnp.exp(-jnp.abs(step_size_in)))
    log_decay = -step_size * column(rate_ref[...])
    row_of = lax.broadcasted_iota(jnp.int32, (BLOCK, BLOCK), 0)
    col_of = lax.broadcasted_iota(jnp.int32, (BLOCK, BLOCK), 1)
    upto = jnp.where(row_of <= col_of, 1.0, 0.0).astype(bf16)
    spread_row = lax.rem(lax.broadcasted_iota(jnp.int32, (2 * heads, chunk), 0), heads)
    spread_col = lax.broadcasted_iota(jnp.int32, (2 * heads, chunk), 1) // head_size

    def lanes_of(c, width):
        if isinstance(c, int):
            return slice(c * width, (c + 1) * width)
        return pl.ds(pl.multiple_of(c * width, width), width)

    def widen(value, c):
        spread = jnp.where(spread_row == spread_col + c * (chunk // head_size), 1.0, 0.0)
        return lax.dot_general(
            value, spread.astype(bf16), (((0,), (0,)), ((), ())), preferred_element_type=f32
        )

    for b in range(blocks):
        at = slice(b * BLOCK, (b + 1) * BLOCK)
        sums = jnp.dot(split(log_decay[:, at], 3), upto, preferred_element_type=f32)
        cumulative = sums[:heads] + sums[heads : 2 * heads] + sums[2 * heads :]
        wide_ref[b, 0] = split(jnp.exp(cumulative), 2)
        wide_ref[b, 1] = split(jnp.exp(-cumulative) * step_size[:, at], 2)

    def open_wide(c):
        lanes = lanes_of(c, chunk)
        decay = 1.0
        for b in range(blocks):
            at = slice(b * BLOCK, (b + 1) * BLOCK)
            grown = widen(wide_ref[b, 0], c)
            grow[at, lanes] = grown
            local_y[at, lanes] = widen(wide_ref[b, 1], c)
            decay = decay * grown[BLOCK - 1 :]
        decay_ref[0:1, lanes] = decay

    for load in loads[3:6]:
        load.wait()
    top = lax.broadcasted_iota(jnp.int32, (EDGE, segment), 0) < EDGE // 2
    turn = lambda value: pltpu.roll(value, EDGE // 2, 0)
    ends = [tail_x[:, i * segment : (i + 1) * segment].astype(f32)[HALO - EDGE :] for i in range(4)]
    halo_out[:, :segment] = jnp.concatenate(
        [jnp.where(top, turn(ends[i]), ends[i + 1]) for i in (0, 2)], axis=0
    ).astype(bf16)
    here = coupling[...].astype(f32)
    for i in range(2):
        pad_bc[EDGE:, i * n : (i + 1) * n] = here[:, i]
    end_b, end_c = pad_bc[rows:, :n], pad_bc[rows:, n:]
    packed = jnp.where(top[:, :n], turn(end_b), end_c)
    halo_out[:, segment:] = jnp.concatenate([packed, packed], axis=0).astype(bf16)

    def conv_one(i, b):
        total = 0.0
        for k in range(taps):
            shift = EDGE - taps + 1 + k + b * BLOCK
            total = total + coupling_taps_ref[k, i : i + 1, :] * (
                pad_bc[shift : shift + BLOCK, i * n : (i + 1) * n]
            )
        return silu(total)

    def open_b(b):
        value = conv_one(0, b)
        b_keep[b] = value.astype(bf16)
        b_turned[b] = value.T.astype(bf16)

    def open_c(b):
        value = conv_one(1, b).astype(bf16)
        scores = lax.dot_general(
            value, b_keep[b], (((1,), (1,)), ((), ())), preferred_element_type=f32
        )
        lhs[b, :, :BLOCK] = jnp.where(row_of >= col_of, scores, 0.0).astype(bf16)
        lhs[b, :, BLOCK:] = value

    def unpack():
        value = halo_in[:, segment:].astype(f32)[:EDGE]
        pad_bc[:EDGE, :n] = turn(value)
        pad_bc[:EDGE, n:] = value
        for i in (0, 2):
            value = halo_in[:, :segment].astype(f32)[i // 2 * EDGE : (i // 2 + 1) * EDGE]
            pad_x[:EDGE, i * segment : (i + 1) * segment] = turn(value)
            pad_x[:EDGE, (i + 1) * segment : (i + 2) * segment] = value

    for b in range(1, blocks):
        open_b(b)
    neighbours = jnp.minimum(ctx, 1) + jnp.minimum(ctx_count - 1 - ctx, 1)
    pl.semaphore_wait(barrier, len(peers) + neighbours)

    halo = pltpu.make_async_remote_copy(
        src_ref=halo_out,
        dst_ref=halo_in,
        send_sem=halo_send,
        recv_sem=halo_recv,
        device_id={"ctx": lax.rem(ctx + 1, ctx_count)},
        device_id_type=MESH,
    )

    @pl.when(ctx < ctx_count - 1)
    def _():
        halo.start()

    def load_rest():
        for load in loads[later:]:
            load.start()

    load_rest()

    def parts(c):
        return [c * (chunk // BLOCK) + i for i in range(chunk // BLOCK)]

    def state_copy(c):
        return pltpu.make_async_remote_copy(
            src_ref=state_out.at[c],
            dst_ref=state_in.at[c],
            send_sem=state_send.at[c],
            recv_sem=state_recv.at[c],
            device_id={"ctx": lax.rem(ctx + 1, ctx_count)},
            device_id_type=MESH,
        )

    def loop(count, body):
        for c in range(count):
            body(c)

    def conv_signal(start, stop, lanes):
        total = 0.0
        for k in range(taps):
            shift = EDGE - taps + 1 + k + start
            total = total + signal_taps_ref[k : k + 1, lanes] * (
                pad_x[shift : shift + stop - start, lanes]
            )
        x_here = silu(total)
        conv_x[start:stop, lanes] = x_here.astype(bf16)
        b = start // BLOCK
        scaled = (x_here * local_y[start:stop, lanes]).astype(bf16)
        rhs[b, start - b * BLOCK : stop - b * BLOCK, lanes] = scaled
        return scaled

    def inside(c):
        lanes = lanes_of(c, chunk)
        loads[signal_at + c].wait()
        open_wide(c)
        pad_x[EDGE:, lanes] = signal[:, lanes].astype(f32)
        for b in range(1, blocks):
            scaled = conv_signal(b * BLOCK, (b + 1) * BLOCK, lanes)
            piece_ref[b - 1, :, lanes] = jnp.dot(b_turned[b], scaled, preferred_element_type=f32)
        conv_signal(HALO, BLOCK, lanes)

    def ahead(c):
        lanes = lanes_of(c, chunk)
        conv_signal(0, HALO, lanes)
        state = jnp.dot(b_turned[0], rhs[0, :BLOCK, lanes], preferred_element_type=f32)
        state = state * grow[block_ends[0] : block_ends[0] + 1, lanes]
        for b in range(1, blocks):
            rhs[b, BLOCK:, lanes] = state.astype(bf16)
            state = (state + piece_ref[b - 1, :, lanes]) * (
                grow[block_ends[b] : block_ends[b] + 1, lanes]
            )
        final[:, lanes] = state

    def send_own(p):
        state_out[p] = final[:, lanes_of(p, BLOCK)].astype(bf16)
        state_copy(p).start()

    loads[6].wait()

    @pl.when(first)
    def _():
        unpack()
        open_b(0)

        def step(c):
            inside(c)
            ahead(c)

            for p in parts(c):
                send_own(p)

        loop(chunks, step)

    @pl.when(ctx > 0)
    def _():
        loop(chunks, inside)

    for load in loads[later + 2 : later + 3] + loads[later + 4 :]:
        load.wait()
    adapter = adapter_ref[0]
    held = down_table.shape[0]
    table_row = lax.rem(adapter, held)
    holder = adapter // held
    tables = []
    for i, (table, out, into) in enumerate(
        ((down_table, down_out, down_in), (up_table, up_out, up_in))
    ):
        width = out.shape[2]
        for dr in range(1, rep_count):
            other = lax.rem(rep + dr, rep_count)
            out[dr - 1] = table[table_row, :, pl.ds(pl.multiple_of(other * width, width), width)]
            copy = pltpu.make_async_remote_copy(
                src_ref=out.at[dr - 1],
                dst_ref=into.at[dr - 1],
                send_sem=table_send.at[i, dr - 1],
                recv_sem=table_recv.at[i, dr - 1],
                device_id={"rep": other},
                device_id_type=MESH,
            )
            copy.start()
            tables.append(copy)

    def forward(p):
        lanes = lanes_of(p, BLOCK)
        state_out[p] = (
            decay_ref[0:1, lanes] * state_in[p].astype(f32) + final[:, lanes]
        ).astype(bf16)
        state_copy(p).start()

    between = jnp.logical_and(ctx > 0, ctx < ctx_count - 1)

    def pass_on(c):
        @pl.when(between)
        def _():
            for p in parts(c):
                state_copy(p).wait_recv()
                forward(p)

    early = min(EARLY, chunks)

    @pl.when(ctx > 0)
    def _():
        halo.wait_recv()
        unpack()
        open_b(0)
        done = 0
        for c in range(early):
            for a in range(done, min(chunks, 2 * c + 1)):
                ahead(a)
            done = max(done, min(chunks, 2 * c + 1))
            pass_on(c)
        for a in range(done, chunks):
            ahead(a)

    for b in range(blocks):
        open_c(b)
    for i in (0, 1, 3):
        loads[later + i].wait()
    skip = lax.dot_general(
        split(jnp.broadcast_to(column(skip_ref[...]), (heads, EDGE)), 2),
        jnp.where(
            lax.rem(lax.broadcasted_iota(jnp.int32, (2 * heads, channels), 0), heads)
            == lax.broadcasted_iota(jnp.int32, (2 * heads, channels), 1) // head_size,
            1.0,
            0.0,
        ).astype(bf16),
        (((0,), (0,)), ((), ())),
        preferred_element_type=f32,
    )[:1]

    for c in range(chunks):
        lanes = slice(c * chunk, (c + 1) * chunk)

        if c + early < chunks:
            pass_on(c + early)

        decay = None
        for b in range(blocks):
            at = slice(b * BLOCK, (b + 1) * BLOCK)
            if b == 0:
                inner = jnp.dot(lhs[b, :, :BLOCK], rhs[b, :BLOCK, lanes], preferred_element_type=f32)
            else:
                inner = jnp.dot(lhs[b], rhs[b, :, lanes], preferred_element_type=f32)
            opened = silu(gate[at, lanes].astype(f32))
            growth = grow[at, lanes]
            y = growth * inner + skip[:, lanes] * conv_x[at, lanes].astype(f32)
            local_y[at, lanes] = y * opened
            end = growth[BLOCK - 1 :]
            spread_growth = growth * opened
            grow[at, lanes] = spread_growth if decay is None else spread_growth * decay
            decay = end if decay is None else decay * end

    for copy in tables:
        copy.wait_recv()

    def chosen(table, into):
        width = into.shape[-1]
        own = table[table_row, :, pl.ds(pl.multiple_of(rep * width, width), width)]
        value = own
        for dr in range(1, rep_count):
            source = lax.rem(rep - dr + rep_count, rep_count)
            here = jnp.full(own.shape, (holder == source).astype(jnp.int32), jnp.int32) > 0
            value = jnp.where(here, into[dr - 1].astype(f32), value.astype(f32)).astype(bf16)
        return value

    down_mine[...] = chosen(down_table, down_in)

    squares = [0.0] * blocks
    low = [0.0] * blocks
    for c in range(chunks):
        lanes = slice(c * chunk, (c + 1) * chunk)

        @pl.when(jnp.logical_and(last, ctx > 0))
        def _():
            for p in parts(c):
                state_copy(p).wait_recv()

        incoming = jnp.concatenate([state_in[p] for p in parts(c)], axis=1)
        for b in range(blocks):
            at = slice(b * BLOCK, (b + 1) * BLOCK)
            carried = jnp.dot(lhs[b, :, BLOCK:], incoming, preferred_element_type=f32)
            gated = local_y[at, lanes] + grow[at, lanes] * carried
            local_y[at, lanes] = gated
            square = gated * gated
            for piece in range(0, chunk, BLOCK):
                squares[b] = squares[b] + square[:, piece : piece + BLOCK]
            gained = (gated * norm_gain_ref[:, lanes]).astype(bf16)
            low[b] = low[b] + lax.dot_general(
                gained, down_mine[:, lanes], (((1,), (1,)), ((), ())), preferred_element_type=f32
            )
    low_own = jnp.concatenate(low, axis=0)
    half = rows // 2
    low_all[0] = jnp.concatenate([low_own[:half], low_own[half:]], axis=1).astype(bf16)
    ones = jnp.ones((EDGE, BLOCK), bf16)
    for b in range(blocks):
        terms = split(squares[b], 2)
        total = lax.dot_general(
            ones, terms, (((1,), (1,)), ((), ())), preferred_element_type=f32
        )
        square_all[0, b : b + 1] = total[:1, :BLOCK] + total[:1, BLOCK:]

    def exchange(slot, dh, dr):
        return [
            pltpu.make_async_remote_copy(
                src_ref=buffer.at[0],
                dst_ref=buffer.at[slot],
                send_sem=send.at[slot],
                recv_sem=recv.at[slot],
                device_id=peer_id(dh, dr),
                device_id_type=MESH,
            )
            for buffer, send, recv in (
                (square_all, square_send, square_recv),
                (low_all, low_send, low_recv),
            )
        ]

    exchanges = [exchange(slot + 1, dh, dr) for slot, (dh, dr) in enumerate(peers)]
    for square_copy, low_copy in exchanges:
        square_copy.start()
    for square_copy, low_copy in exchanges:
        low_copy.start()

    up_mine[...] = chosen(up_table, up_in)

    def inverse_of(dh):
        total = 0.0
        for dr in range(rep_count):
            total = total + square_all[dh * rep_count + dr]
        value = lax.rsqrt(total / (channels * rep_count) + epsilon)
        value = split(value, 3)
        out = []
        for b in range(blocks):
            mine = lax.broadcasted_iota(jnp.int32, value.shape[:1] + (BLOCK,), 0)
            mine = jnp.where(lax.rem(mine, total.shape[0]) == b, 1.0, 0.0).astype(bf16)
            out.append(
                lax.dot_general(
                    value, mine, (((0,), (0,)), ((), ())), preferred_element_type=f32
                )
            )
        return out

    for slot, (dh, dr) in enumerate(peers):
        if dh == 0:
            exchanges[slot][0].wait_recv()
    own_inverse = inverse_of(0)
    for c in range(channels // BLOCK):
        lanes = slice(c * BLOCK, (c + 1) * BLOCK)
        for b in range(blocks):
            at = slice(b * BLOCK, (b + 1) * BLOCK)
            mixer_ref[at, lanes] = (
                local_y[at, lanes] * own_inverse[b] * norm_gain_ref[:, lanes]
            ).astype(bf16)

    for slot, (dh, dr) in enumerate(peers):
        if dh > 0:
            exchanges[slot][0].wait_recv()
        exchanges[slot][1].wait_recv()
    reduced = 0.0
    for dh in range(head_count):
        inverse = own_inverse if dh == 0 else inverse_of(dh)
        inverse = jnp.concatenate(inverse, axis=0)[:, :rank]
        packed = 0.0
        for dr in range(rep_count):
            packed = packed + low_all[dh * rep_count + dr].astype(f32)
        reduced = reduced + inverse * jnp.concatenate([packed[:, :rank], packed[:, rank:]], axis=0)
    reduced_ref[...] = reduced.astype(bf16)

    for copy in tables:
        copy.wait_send()
    for pair in exchanges:
        for copy in pair:
            copy.wait_send()

    @pl.when(ctx < ctx_count - 1)
    def _():
        halo.wait_send()
        for p in range(channels // BLOCK):
            state_copy(p).wait_send()


def finish(mixer_ref, reduced_ref, up_ref, mixer_hbm, delta_hbm, delta, sem):
    rows, width = delta.shape
    mixer_copy = pltpu.make_async_copy(mixer_ref, mixer_hbm, sem.at[0])
    mixer_copy.start()
    step = width // PARTS
    copies = [mixer_copy]
    reduced = reduced_ref[...]
    for c in range(PARTS):
        lanes = pl.ds(c * step, step)
        delta[:, lanes] = jnp.dot(
            reduced, up_ref[:, lanes], preferred_element_type=jnp.float32
        ).astype(jnp.bfloat16)
        copy = pltpu.make_async_copy(delta.at[:, lanes], delta_hbm.at[:, lanes], sem.at[c + 1])
        copy.start()
        copies.append(copy)
    for copy in copies:
        copy.wait()


def local(
    axis_sizes,
    signal_input,
    gate_input,
    coupling_input,
    step_input,
    signal_taps,
    coupling_taps,
    step_bias,
    head_decay_rate,
    head_skip_gain,
    gated_norm_gain,
    request_adapter,
    stored_down_weight,
    stored_up_weight,
):
    ctx_count, head_count, rep_count = axis_sizes
    rows, channels = signal_input.shape
    n = coupling_input.shape[2]
    heads = step_input.shape[0]
    held, rank, down_width = stored_down_weight.shape
    up_width = stored_up_weight.shape[2] // rep_count
    chunk = 256
    pieces = channels // BLOCK
    blocks = rows // BLOCK
    devices = head_count * rep_count
    f32, bf16 = jnp.float32, jnp.bfloat16
    vmem = pl.BlockSpec(memory_space=pltpu.VMEM)
    hbm = pl.BlockSpec(memory_space=pltpu.HBM)
    dma = pltpu.SemaphoreType.DMA
    mixed, reduced, up_mine = pl.pallas_call(
        functools.partial(kernel, (ctx_count, head_count, rep_count, chunk)),
        out_shape=(
            pltpu.VMEM((rows, channels), bf16),
            pltpu.VMEM((rows, rank), bf16),
            pltpu.VMEM((rank, up_width), bf16),
        ),
        in_specs=[hbm] * 13,
        out_specs=(vmem, vmem, vmem),
        scratch_shapes=[
            pltpu.VMEM((rows, channels), bf16),
            pltpu.VMEM((rows, channels), bf16),
            pltpu.VMEM((rows, 2, n), bf16),
            pltpu.VMEM(stored_down_weight.shape, bf16),
            pltpu.VMEM(stored_up_weight.shape, bf16),
            pltpu.VMEM((HALO, channels), bf16),
            pltpu.VMEM((HALO, channels // 4 + n), bf16),
            pltpu.VMEM((HALO, channels // 4 + n), bf16),
            pltpu.VMEM((EDGE + rows, channels), f32),
            pltpu.VMEM((EDGE + rows, 2 * n), f32),
            pltpu.VMEM((rows, channels), bf16),
            pltpu.VMEM((blocks, BLOCK + n, channels), bf16),
            pltpu.VMEM((blocks, BLOCK, BLOCK + n), bf16),
            pltpu.VMEM((blocks, n, BLOCK), bf16),
            pltpu.VMEM((rows, channels), f32),
            pltpu.VMEM((rows, channels), f32),
            pltpu.VMEM((n, channels), f32),
            pltpu.VMEM((max(blocks - 1, 1), n, channels), f32),
            pltpu.VMEM((blocks, BLOCK, n), bf16),
            pltpu.VMEM((blocks, 2, 2 * heads, BLOCK), bf16),
            pltpu.VMEM((8, channels), f32),
            pltpu.SMEM((1,), jnp.int32),
            pltpu.VMEM((pieces, n, BLOCK), bf16),
            pltpu.VMEM((pieces, n, BLOCK), bf16),
            pltpu.VMEM((rep_count - 1, rank, channels), bf16),
            pltpu.VMEM((rep_count - 1, rank, channels), bf16),
            pltpu.VMEM((rank, channels), bf16),
            pltpu.VMEM((rep_count - 1, rank, up_width), bf16),
            pltpu.VMEM((rep_count - 1, rank, up_width), bf16),
            pltpu.VMEM((devices, rows // 2, 2 * rank), bf16),
            pltpu.VMEM((devices, -(-blocks // EDGE) * EDGE, BLOCK), f32),
            pltpu.VMEM(step_input.shape, f32),
            pltpu.VMEM(signal_taps.shape, f32),
            pltpu.VMEM(coupling_taps.shape, f32),
            pltpu.VMEM((1, heads), f32),
            pltpu.VMEM((1, heads), f32),
            pltpu.VMEM((1, heads), f32),
            pltpu.VMEM((1, channels), f32),
            dma((13 + channels // chunk,)),
            dma,
            dma,
            dma((2, rep_count - 1)),
            dma((2, rep_count - 1)),
            dma((pieces,)),
            dma((pieces,)),
            dma((devices,)),
            dma((devices,)),
            dma((devices,)),
            dma((devices,)),
        ],
        compiler_params=pltpu.CompilerParams(
            collective_id=0, has_side_effects=True, vmem_limit_bytes=62500000
        ),
    )(
        request_adapter,
        signal_input,
        gate_input,
        coupling_input,
        stored_down_weight,
        stored_up_weight,
        step_input,
        signal_taps,
        coupling_taps,
        step_bias.reshape(1, -1),
        head_decay_rate.reshape(1, -1),
        head_skip_gain.reshape(1, -1),
        gated_norm_gain.reshape(1, -1),
    )
    return pl.pallas_call(
        finish,
        out_shape=(
            jax.ShapeDtypeStruct((rows, channels), bf16),
            jax.ShapeDtypeStruct((rows, up_width), bf16),
        ),
        in_specs=[vmem, vmem, vmem],
        out_specs=(hbm, hbm),
        scratch_shapes=[pltpu.VMEM((rows, up_width), bf16), dma((PARTS + 1,))],
        compiler_params=pltpu.CompilerParams(vmem_limit_bytes=8000000),
    )(mixed, reduced, up_mine)


def solution(mesh):
    in_specs = (
        P(("group", "ctx"), ("head", "rep")),
        P(("group", "ctx"), ("head", "rep")),
        P(("group", "ctx"), None, "head"),
        P(("head", "rep"), ("group", "ctx")),
        P(None, ("head", "rep")),
        P(None, None, "head"),
        P(("head", "rep")),
        P(("head", "rep")),
        P(("head", "rep")),
        P(("head", "rep")),
        P("group"),
        P("rep", None, "head"),
        P("rep", None, "head"),
    )
    out_specs = (P(("group", "ctx"), ("head", "rep")), P(("group", "ctx"), ("head", "rep")))
    axis_sizes = tuple(mesh.shape[name] for name in ("ctx", "head", "rep"))
    return jax.shard_map(
        functools.partial(local, axis_sizes),
        mesh=mesh,
        in_specs=in_specs,
        out_specs=out_specs,
        check_vma=False,
    )
```
